512 devices in a mesh: row: 64 (over y, x, core), col: 8 (over z).
Axes of the slice: x: 4, y: 8, z: 8, core: 2. Of those that a mesh axis runs over, the one named last changes fastest.
Arguments:
- hamiltonian: float32 [24576, 24576], P('row', 'col'), as said below
- previous: float32 [24576, 56], P('row', 'col'), may hold values from -6 to 6
- correlation_map: int32 [24576], P('row'), may hold values from 0 to 24575, each once
- lower_cut: float32 [1], replicated, may hold values from 0.5 to 1.5
- upper_bound: float32 [1], replicated, may hold values from 5.5 to 6.5
Outputs:
- basis_out: float32 [24576, 56], P('row', 'col')
- ritz_matrix: float32 [56, 56], replicated
The draws below stay inside these ranges and needn't reach their ends.
Inputs may be any that keep to these rules, and one draw needn't show every extreme that they name: correlation_map names every index of 0 .. 24575 exactly once. hamiltonian is symmetric.
All inputs are finite; a program needn't handle non-finite values.
Results may differ from the reference program's by a relative error of at most 0.00013.
Values sent between devices are 32-bit elements; how exact they have to be, the bound alone decides.
A program may use at most 64 MiB of HBM per device.

```python
import math
import jax
import jax.numpy as jnp
from jax import lax

N = 24576
K = 56
DEG = 4


def draw_hamiltonian(key, part):
    key_coupling = jax.random.fold_in(key, 11)
    key_potential = jax.random.fold_in(key, 12)
    coupling = jax.random.normal(key_coupling, (N, N), jnp.float32)
    symmetric = (coupling + coupling.T) * (math.sqrt(0.5) / math.sqrt(N))
    position = jnp.arange(N, dtype=jnp.float32) / N
    potential = 3.0 * position + jax.random.uniform(key_potential, (N,), jnp.float32, 0.0, 1.5)
    return symmetric + jnp.diag(potential)


def shard_levels(rng, dims, shards, low, largest):
    gain = 1.0
    for dim, shards_of in shards:
        steps = jax.random.uniform(jax.random.fold_in(jax.random.fold_in(rng, 6), dim), (shards_of,), jnp.float32, low / len(shards), largest / len(shards))
        gain = gain * jnp.repeat(jnp.exp(steps), dims[dim] // shards_of).reshape((-1,) + (1,) * (len(dims) - 1 - dim))
    return gain


def bell_draw(own_key, extent, width, bound, pieces=(), kind=jnp.bfloat16):
    array = jax.random.normal(own_key, extent, jnp.float32) * width
    if len(pieces) > 0:
        array = shard_levels(own_key, extent, pieces, -0.22, 0.18) * array
    return jnp.clip(array, min=-bound, max=bound).astype(kind)


def setup_inputs(seed: int = 0) -> dict:
    splits = jax.random.split(jax.random.key(seed), 6)
    return {
        "hamiltonian": draw_hamiltonian(jax.random.fold_in(splits[5], 71), 0),
        "previous": bell_draw(splits[1], (N, K), 1.0, 6.0, ((0, 64), (1, 8)), jnp.float32),
        "correlation_map": jax.random.permutation(splits[2], N).astype(jnp.int32),
        "lower_cut": jnp.clip(jax.random.uniform(splits[3], (1,), jnp.float32, 0.5, 1.5), 0.5, 1.5),
        "upper_bound": jnp.clip(jax.random.uniform(splits[4], (1,), jnp.float32, 5.5, 6.5), 5.5, 6.5),
    }


def reference(hamiltonian, previous, correlation_map, lower_cut, upper_bound):
    centre = (upper_bound[0] + lower_cut[0]) * 0.5
    half_width = (upper_bound[0] - lower_cut[0]) * 0.5

    def operate_on(vectors):
        return jnp.dot(hamiltonian, vectors, precision=lax.Precision.HIGHEST)
    earlier = jnp.take(previous, correlation_map.astype(jnp.int32), axis=0)
    current = (operate_on(earlier) - centre * earlier) / half_width
    for repeat in range(DEG - 1):
        following = 2.0 * (operate_on(current) - centre * current) / half_width - earlier
        earlier = current
        current = following
    applied = operate_on(current)
    gram_matrix = jnp.dot(current.T, current, precision=lax.Precision.HIGHEST) / N
    projected = jnp.dot(current.T, applied, precision=lax.Precision.HIGHEST) / N
    factor = jnp.linalg.cholesky(gram_matrix)
    identity = jnp.eye(K, dtype=factor.dtype)
    inverse = lax.linalg.triangular_solve(factor, identity, left_side=True, lower=True)
    basis_out = jnp.dot(current, inverse.T, precision=lax.Precision.HIGHEST)
    ritz_matrix = jnp.dot(jnp.dot(inverse, projected, precision=lax.Precision.HIGHEST), inverse.T, precision=lax.Precision.HIGHEST)
    return (basis_out, ritz_matrix)
```

```python
import jax
import jax.numpy as jnp
from jax import lax
from jax.experimental import pallas as pl
from jax.experimental.pallas import tpu as pltpu
from jax.sharding import PartitionSpec as P

MESH = pl.DeviceIdType.MESH
F32 = jnp.float32
BF16 = jnp.bfloat16
HIGHEST = lax.Precision.HIGHEST
NSEM = 224


def far_first(n):
    return sorted(range(1, n), key=lambda d: -min(d, n - d))


def pick(k, table):
    return sum((k == i).astype(jnp.int32) * t for i, t in enumerate(table) if t)


def nt(a, b):
    return lax.dot_general(a, b, (((1,), (1,)), ((), ())), precision=HIGHEST, preferred_element_type=F32)


def kernel(
    X, Y, Z, RB, K, N,
    h_hbm, pk, idx, amod, lo, up,
    basis_ref, ritz_ref,
    hf, hcat, pall, picked, z0, xr0, lhs, acc, qb, cb, sb, xb, ysum, yb, XC, f1,
    zsum, zb, XR, f2, XT, gst, gy, gx, gc, gz, pst, pz, px, pc, py, inv_ref,
    hsem, ssem, rsem,
):
    G = K // 8
    W = K // Z
    PR = RB // 16
    r = lax.axis_index("row")
    z = lax.axis_index("col")
    core = lax.rem(r, 2)
    x = lax.rem(r // 2, X)
    y = r // (2 * X)
    other = 1 - core

    def dev(x_, y_, c_, z_):
        return ((y_ * X + x_) * 2 + c_, z_)

    zdev = lambda q: dev(x, y, core, q)
    ydev = lambda q: dev(x, q, core, z)
    xdev = lambda q: dev(q, y, core, z)
    partner = dev(x, y, other, z)
    swap = dev(x, z, core, y)

    used = [0]
    drains = []

    def alloc(n):
        base = used[0]
        used[0] += n
        assert used[0] <= NSEM
        return base

    def rc(src, dst, si, ri, to):
        return pltpu.make_async_remote_copy(
            src_ref=src, dst_ref=dst, send_sem=ssem.at[si], recv_sem=rsem.at[ri], device_id=to, device_id_type=MESH
        )

    class Axis:
        def __init__(self, n, me, devof, owners):
            self.n, self.me, self.devof, self.owners = n, me, devof, owners
            self.base = alloc(n)

        def guarded(self, who, fn):
            if self.owners >= self.n:
                fn()
            else:
                pl.when(who < self.owners)(fn)

        def ahead(self, d):
            return lax.rem(self.me + d, self.n)

        def behind(self, d):
            return lax.rem(self.me + self.n - d, self.n)

        def spread(self, at):
            def go():
                for d in far_first(self.n):
                    rc(at(self.me), at(self.me), self.base + d, self.base + self.me, self.devof(self.ahead(d))).start()

            self.guarded(self.me, go)

            def drain():
                def fin():
                    for d in far_first(self.n):
                        rc(at(self.me), at(self.me), self.base + d, self.base + self.me, self.devof(self.ahead(d))).wait_send()

                self.guarded(self.me, fin)

            drains.append(drain)

        def gathered(self, at):
            for d in reversed(far_first(self.n)):
                q = self.behind(d)

                def fin(d=d, q=q):
                    rc(at(q), at(q), self.base + d, self.base + q, self.devof(q)).wait_recv()

                self.guarded(q, fin)

        def scatter(self, src, dst):
            def each(method):
                for d in far_first(self.n):
                    p = self.ahead(d)

                    def go(d=d, p=p):
                        getattr(rc(src(p), dst(self.me), self.base + d, self.base + self.me, self.devof(p)), method)()

                    self.guarded(p, go)

            each("start")
            drains.append(lambda: each("wait_send"))

        def scattered(self, dst):
            for d in reversed(far_first(self.n)):
                q = self.behind(d)
                rc(dst(q), dst(q), self.base + d, self.base + q, self.devof(q)).wait_recv()

    hload = [pltpu.make_async_copy(h_hbm.at[:, pl.ds(i * 2 * RB, 2 * RB)], hf.at[i], hsem.at[i]) for i in range(X)]
    for c in hload:
        c.start()

    barrier = pltpu.get_barrier_semaphore()

    def greet(to):
        pl.semaphore_signal(barrier, inc=1, device_id=to, device_id_type=MESH)

    for d in range(1, Z):
        greet(zdev(lax.rem(z + d, Z)))
    for d in range(1, Y):
        greet(ydev(lax.rem(y + d, Y)))
    for d in range(1, X):
        greet(xdev(lax.rem(x + d, X)))
    greet(partner)

    @pl.when(y != z)
    def _():
        greet(swap)

    pl.semaphore_wait(barrier, (Z - 1) + (Y - 1) + (X - 1) + 1 + (y != z).astype(jnp.int32))

    centre = (up[0] + lo[0]) * 0.5
    half_width = (up[0] - lo[0]) * 0.5
    inv_hw = 1.0 / half_width

    def prow(x_, c_, y_):
        return pall.at[pl.ds(pl.multiple_of(((x_ * 2 + c_) * Y + y_) * PR, 8), PR)]

    def pblk(x_, c_):
        return pall.at[pl.ds(pl.multiple_of((x_ * 2 + c_) * Y * PR, 8), Y * PR)]

    class Plane:
        def __init__(self, blk):
            self.xa = Axis(X, x, xdev, X)
            self.cbase = alloc(X)
            self.blk = blk

        def to_partner(self, q, method):
            getattr(rc(self.blk(q, core), self.blk(q, core), self.cbase + q, self.cbase + q, partner), method)()

        def start(self):
            self.xa.spread(lambda q: self.blk(q, core))
            self.to_partner(x, "start")

        def relay(self):
            for d in reversed(far_first(X)):
                q = self.xa.behind(d)
                rc(self.blk(q, core), self.blk(q, core), self.xa.base + d, self.xa.base + q, xdev(q)).wait_recv()
                self.to_partner(q, "start")

            def drain():
                for q in range(X):
                    self.to_partner(q, "wait_send")

            drains.append(drain)

        def other_half(self, q):
            rc(self.blk(q, other), self.blk(q, other), self.cbase + q, self.cbase + q, partner).wait_recv()

    def split_h(i):
        hload[i].wait()
        diagonal = (y == z).astype(jnp.int32) * (x == i).astype(jnp.int32)
        off = core * RB - (1 - diagonal) * (8 * RB)

        hfi, hci = hf.at[i], hcat.at[i]

        @pl.loop(0, RB // 16)
        def _(t):
            row = pl.multiple_of(t * 16, 16)
            h = hfi[pl.ds(row, 16), :]
            ri = lax.broadcasted_iota(jnp.int32, h.shape, 0) + row
            ci = lax.broadcasted_iota(jnp.int32, h.shape, 1)
            h = jnp.where(ci - ri == off, h - centre, h)
            hi = h.astype(BF16)
            hci[pl.ds(row, 16), :] = hi
            hci[pl.ds(pl.multiple_of(row + RB, 16), 16), :] = (h - hi.astype(F32)).astype(BF16)

    prow(x, core, y)[...] = pk[...]
    s0y = Axis(Y, y, ydev, Y)
    s0y.spread(lambda q: prow(x, core, q))
    for i in range(X // 2):
        split_h(i)
    s0y.gathered(lambda q: prow(x, core, q))
    s0p = Plane(pblk)
    s0p.start()
    for i in range(X // 2, X):
        split_h(i)
    s0p.relay()
    for q in range(X):
        s0p.other_half(q)

    @pl.loop(0, RB // 8)
    def _(t):
        for u in range(8):
            picked[pl.ds(t * 8 + u, 1), :] = pall[pl.ds(idx[t * 8 + u], 1), :]

    lane = lax.broadcasted_iota(jnp.int32, (RB, 128), 1)
    mine = jnp.where(lane // 8 == amod[...], picked[...], 0.0)
    fold = (lax.broadcasted_iota(jnp.int32, (8, 128), 1) % 8 == lax.broadcasted_iota(jnp.int32, (8, 128), 0)).astype(F32)
    z0[z] = nt(fold, mine)
    s1 = Axis(Z, z, zdev, Z)
    s1.spread(lambda q: z0.at[q])
    s1.gathered(lambda q: z0.at[q])
    for g in range(Z):
        xr0[pl.ds(g * W, W), :] = z0[g][:W, :]

    def cat(v):
        hi = v.astype(BF16).astype(F32)
        return jnp.concatenate([hi, v - hi], axis=0).astype(BF16)

    dxs = far_first(X)

    class Wide:
        def __init__(self, i):
            self.i = i
            self.cbase = alloc(X)
            self.xa = Axis(X, x, xdev, X)
            self.ya = Axis(Y, y, ydev, G)

        def pc(self, q, method):
            i = self.i
            getattr(rc(qb.at[i, q, other], cb.at[i, q], self.cbase + q, self.cbase + q, partner), method)()

        def multiply(self, v):
            i = self.i
            c2 = cat(v)
            lhs[:, :RB] = c2
            lhs[:, RB:] = c2

            @pl.loop(0, X)
            def _(k):
                q = lax.rem(x + pick(k, dxs + [0]), X)
                p = jnp.dot(lhs[...], hcat[q], preferred_element_type=F32)
                p = p[:K] + p[K:]
                qb[i, q, 0] = p[:, :RB].reshape(G, 8, RB)
                qb[i, q, 1] = p[:, RB:].reshape(G, 8, RB)
                self.pc(q, "start")

            drains.append(lambda: [self.pc(q, "wait_send") for q in range(X)])

        def pair(self, q):
            i = self.i
            rc(cb.at[i, q], cb.at[i, q], self.cbase + q, self.cbase + q, partner).wait_recv()
            return qb[i, q, core] + cb[i, q]

        def across(self):
            i, xa = self.i, self.xa

            def cp(d):
                q = xa.ahead(d)
                return rc(sb.at[i, q], xb.at[i, x], xa.base + d, xa.base + x, xdev(q))

            for d in dxs:
                q = xa.ahead(d)
                sb[i, q] = self.pair(q)
                cp(d).start()
            drains.append(lambda: [cp(d).wait_send() for d in dxs])

        def down(self):
            i = self.i
            total = self.pair(x)
            self.xa.scattered(lambda q: xb.at[i, q])
            for d in dxs:
                total = total + xb[i, self.xa.behind(d)]
            ysum[i] = total
            self.ya.scatter(lambda q: ysum.at[i, q], lambda q: yb.at[i, q])

        def chunk(self):
            i = self.i
            yb[i, y] = ysum[i, y]
            self.ya.scattered(lambda q: yb.at[i, q])
            total = yb[i, 0]
            for q in range(1, Y):
                total = total + yb[i, q]
            return total

    class Gather:
        def __init__(self, i):
            self.i = i
            self.ya = Axis(Y, y, ydev, G)
            self.plane = Plane(lambda q, c: XC.at[i, q, c])

        def run(self):
            i = self.i
            self.ya.spread(lambda q: XC.at[i, x, core, q])
            self.ya.gathered(lambda q: XC.at[i, x, core, q])
            self.plane.start()
            self.plane.relay()

    class Tall:
        def __init__(self, i):
            self.i = i
            self.rs = Axis(Z, z, zdev, G)
            self.ag = Axis(Z, z, zdev, G)

        def multiply(self, plane):
            i = self.i
            acc[...] = jnp.zeros_like(acc)

            @pl.loop(0, X)
            def _(k):
                q = lax.rem(x + pick(k, [0] + dxs[::-1]), X)
                plane.other_half(q)
                v = jnp.concatenate([XC[i, q, 0].reshape(K, RB), XC[i, q, 1].reshape(K, RB)], axis=1)
                acc[...] += lax.dot_general(cat(v), hcat[q], (((1,), (1,)), ((), ())), preferred_element_type=F32)

            a = acc[...]
            t = a[:K] + a[K:]
            t = t[:, :RB] + t[:, RB:]
            zsum[i] = t.reshape(G, 8, RB)
            self.rs.scatter(lambda q: zsum.at[i, q], lambda q: zb.at[i, q])

        def chunk(self):
            i = self.i
            zb[i, z] = zsum[i, z]
            self.rs.scattered(lambda q: zb.at[i, q])
            total = zb[i, 0]
            for q in range(1, Z):
                total = total + zb[i, q]
            return total

        def run(self):
            i = self.i
            self.ag.spread(lambda q: XR.at[i, q])
            self.ag.gathered(lambda q: XR.at[i, q])

    w0, w1, w2 = Wide(0), Wide(1), Wide(2)
    g0, g1 = Gather(0), Gather(1)
    t0, t1 = Tall(0), Tall(1)

    w0.multiply(xr0[...])
    w0.across()
    w0.down()

    @pl.when(y < G)
    def _():
        v = w0.chunk() * inv_hw
        f1[...] = v
        XC[0, x, core, y] = v

    g0.run()
    t0.multiply(g0.plane)

    @pl.when(z < G)
    def _():
        v = 2.0 * inv_hw * t0.chunk() - xr0[pl.ds(pl.multiple_of(z * 8, 8), 8), :]
        f2[...] = v
        XR[0, z] = v

    t0.run()
    w1.multiply(XR[0].reshape(K, RB))
    w1.across()
    w1.down()

    @pl.when(y < G)
    def _():
        XC[1, x, core, y] = 2.0 * inv_hw * w1.chunk() - f1[...]

    g1.run()
    t1.multiply(g1.plane)

    @pl.when(z < G)
    def _():
        XR[1, z] = 2.0 * inv_hw * t1.chunk() - f2[...]

    t1.run()

    tb = alloc(1)

    def turn(method):
        @pl.when(y != z)
        def _():
            getattr(rc(XR.at[1], XT, tb, tb, swap), method)()

    turn("start")
    drains.append(lambda: turn("wait_send"))
    w2.multiply(XR[1].reshape(K, RB))

    gay, gax, gaz = Axis(Y, y, ydev, Y), Axis(X, x, xdev, X), Axis(Z, z, zdev, G)
    paz, pax, pay = Axis(Z, z, zdev, Z), Axis(X, x, xdev, X), Axis(Y, y, ydev, G)
    gcb, pcb = alloc(1), alloc(1)

    def widen(v):
        return jnp.concatenate([v, jnp.zeros((8, 128 - K), F32)], axis=1)

    class Guard:
        def __init__(self, cond):
            self.cond = cond

        def __call__(self, fn):
            before = len(drains)
            pl.when(self.cond)(fn)
            late = drains[before:]
            del drains[before:]

            def drain():
                def fin():
                    for f in late:
                        f()

                pl.when(self.cond)(fin)

            drains.append(drain)

    gown, pown = Guard(z < G), Guard(y < G)

    def total_of(ref, n):
        t = ref[0]
        for q in range(1, n):
            t = t + ref[q]
        return t

    def swap_cores(ref, base):
        cp = lambda: rc(ref.at[core], ref.at[core], base, base, partner)
        cp().start()
        drains.append(lambda: cp().wait_send())

    def swapped(ref, base):
        rc(ref.at[other], ref.at[other], base, base, partner).wait_recv()

    @gown
    def _():
        gy[y] = widen(nt(XR[1, z], XR[1].reshape(K, RB)))
        gay.spread(lambda q: gy.at[q])

    w2.across()

    @gown
    def _():
        gay.gathered(lambda q: gy.at[q])
        gx[x] = total_of(gy, Y)
        gax.spread(lambda q: gx.at[q])

    w2.down()

    @gown
    def _():
        gax.gathered(lambda q: gx.at[q])
        gc[core] = total_of(gx, X)
        swap_cores(gc, gcb)

    @pl.when(y != z)
    def _():
        rc(XT, XT, tb, tb, swap).wait_recv()

    @pl.when(y == z)
    def _():
        XT[...] = XR[1]

    @pown
    def _():
        pz[z] = widen(nt(w2.chunk(), XT[...].reshape(K, RB)))
        paz.spread(lambda q: pz.at[q])

    @gown
    def _():
        swapped(gc, gcb)
        gz[z] = gc[0] + gc[1]

    gaz.spread(lambda q: gz.at[q])

    @pown
    def _():
        paz.gathered(lambda q: pz.at[q])
        px[x] = total_of(pz, Z)
        pax.spread(lambda q: px.at[q])

    gaz.gathered(lambda q: gz.at[q])
    gram = gz[...].reshape(K, 128)[:, :K] * (1.0 / N)

    eye = (lax.broadcasted_iota(jnp.int32, (K, K), 0) == lax.broadcasted_iota(jnp.int32, (K, K), 1)).astype(F32)
    work = jnp.concatenate([gram, eye], axis=1)
    rows = lax.broadcasted_iota(jnp.int32, (K, 1), 0)
    scale = jnp.zeros((K, 1), F32)

    def eliminate(first, last, work, scale):
        for j in range(first, last):
            prow_ = work[j : j + 1, :]
            piv = work[j : j + 1, j : j + 1]
            col = work[:, j : j + 1]
            m = jnp.where(rows > j, col / piv, 0.0)
            scale = jnp.where(rows == j, piv, scale)
            work = work - m * prow_
        return work, scale

    work, scale = eliminate(0, K // 3, work, scale)

    @pown
    def _():
        pax.gathered(lambda q: px.at[q])
        pc[core] = total_of(px, X)
        swap_cores(pc, pcb)

    work, scale = eliminate(K // 3, K // 2, work, scale)

    @pown
    def _():
        swapped(pc, pcb)
        py[y] = pc[0] + pc[1]

    pay.spread(lambda q: py.at[q])
    work, scale = eliminate(K // 2, K, work, scale)
    inverse = work[:, K:] * lax.rsqrt(scale)
    inv_ref[...] = inverse
    own = inv_ref[pl.ds(z * W, W), :]
    basis_ref[...] = jnp.dot(own, XR[1].reshape(K, RB), precision=HIGHEST, preferred_element_type=F32)

    pay.gathered(lambda q: py.at[q])
    proj = py[...].reshape(K, 128)[:, :K] * (1.0 / N)
    proj = proj + centre * gram
    ritz_ref[...] = nt(nt(inverse, proj), inverse)

    for f in drains:
        f()


def body(hamiltonian, previous, correlation_map, lower_cut, upper_bound):
    Z = lax.axis_size("col")
    R = lax.axis_size("row")
    Y = Z
    X = R // (2 * Y)
    RB, W = previous.shape
    K = W * Z
    G = K // 8
    N = RB * R
    PR = RB // 16
    pk = jnp.pad(previous, ((0, 0), (0, 8 - W))).reshape(PR, 128)
    src = correlation_map // RB
    off = correlation_map % RB
    slot = (src % (2 * X)) * Y + src // (2 * X)
    idx = slot * PR + off // 16
    amod = (off % 16)[:, None]
    V, S = pltpu.VMEM, pltpu.SMEM
    blk = (G, 8, RB)
    scratch = [
        V((X, RB, 2 * RB), F32),
        V((X, 2 * RB, 2 * RB), BF16),
        V((R * PR, 128), F32),
        V((RB, 128), F32),
        V((Z, 8, RB), F32),
        V((K, RB), F32),
        V((2 * K, 2 * RB), BF16),
        V((2 * K, 2 * RB), F32),
        V((3, X, 2) + blk, F32),
        V((3, X) + blk, F32),
        V((3, X) + blk, F32),
        V((3, X) + blk, F32),
        V((3,) + blk, F32),
        V((3, Y, 8, RB), F32),
        V((2, X, 2) + blk, F32),
        V((8, RB), F32),
        V((2,) + blk, F32),
        V((2, Z, 8, RB), F32),
        V((2,) + blk, F32),
        V((8, RB), F32),
        V(blk, F32),
        V((8, 128), F32),
        V((Y, 8, 128), F32),
        V((X, 8, 128), F32),
        V((2, 8, 128), F32),
        V((G, 8, 128), F32),
        V((8, 128), F32),
        V((Z, 8, 128), F32),
        V((X, 8, 128), F32),
        V((2, 8, 128), F32),
        V((G, 8, 128), F32),
        V((K, K), F32),
        pltpu.SemaphoreType.DMA((X,)),
        pltpu.SemaphoreType.DMA((NSEM,)),
        pltpu.SemaphoreType.DMA((NSEM,)),
    ]
    vm = pl.BlockSpec(memory_space=V)
    sm = pl.BlockSpec(memory_space=S)
    basis_t, ritz = pl.pallas_call(
        lambda *refs: kernel(X, Y, Z, RB, K, N, *refs),
        out_shape=(jax.ShapeDtypeStruct((W, RB), F32), jax.ShapeDtypeStruct((K, K), F32)),
        in_specs=[pl.BlockSpec(memory_space=pl.ANY), vm, sm, vm, sm, sm],
        out_specs=(vm, vm),
        scratch_shapes=scratch,
        compiler_params=pltpu.CompilerParams(collective_id=0, has_side_effects=True, vmem_limit_bytes=60 * 1024 * 1024),
        name="subspace",
    )(hamiltonian, pk, idx, amod, lower_cut, upper_bound)
    return basis_t.T, ritz


def solution(mesh):
    return jax.shard_map(
        body,
        mesh=mesh,
        in_specs=(P("row", "col"), P("row", "col"), P("row"), P(), P()),
        out_specs=(P("row", "col"), P()),
        check_vma=False,
    )
```

```python
import jax
import jax.numpy as jnp
from jax import lax
from jax.experimental import pallas as pl
from jax.experimental.pallas import tpu as pltpu
from jax.sharding import PartitionSpec as P

MESH = pl.DeviceIdType.MESH
F32 = jnp.float32
BF16 = jnp.bfloat16
HIGHEST = lax.Precision.HIGHEST
NSEM = 224


def far_first(n):
    return sorted(range(1, n), key=lambda d: -min(d, n - d))


def pick(k, table):
    return sum((k == i).astype(jnp.int32) * t for i, t in enumerate(table) if t)


def nt(a, b):
    return lax.dot_general(a, b, (((1,), (1,)), ((), ())), precision=HIGHEST, preferred_element_type=F32)


def kernel(
    X, Y, Z, RB, K, N,
    h_hbm, pk, idx, amod, lo, up,
    basis_ref, ritz_ref,
    hf, hcat, pall, picked, z0, xr0, lhs, acc, qb, cb, sb, xb, ysum, yb, XC, f1,
    zsum, zb, XR, f2, XT, yt, gy, gx, gc, gz, pz, px, pc, py, inv_ref,
    hsem, ssem, rsem,
):
    G = K // 8
    W = K // Z
    PR = RB // 16
    r = lax.axis_index("row")
    z = lax.axis_index("col")
    core = lax.rem(r, 2)
    x = lax.rem(r // 2, X)
    y = r // (2 * X)
    other = 1 - core

    def dev(x_, y_, c_, z_):
        return ((y_ * X + x_) * 2 + c_, z_)

    zdev = lambda q: dev(x, y, core, q)
    ydev = lambda q: dev(x, q, core, z)
    xdev = lambda q: dev(q, y, core, z)
    partner = dev(x, y, other, z)

    used = [0]
    drains = []

    def alloc(n):
        base = used[0]
        used[0] += n
        assert used[0] <= NSEM
        return base

    def rc(src, dst, si, ri, to):
        return pltpu.make_async_remote_copy(
            src_ref=src, dst_ref=dst, send_sem=ssem.at[si], recv_sem=rsem.at[ri], device_id=to, device_id_type=MESH
        )

    class Axis:
        def __init__(self, n, me, devof, owners):
            self.n, self.me, self.devof, self.owners = n, me, devof, owners
            self.base = alloc(n)

        def guarded(self, who, fn):
            if self.owners >= self.n:
                fn()
            else:
                pl.when(who < self.owners)(fn)

        def ahead(self, d):
            return lax.rem(self.me + d, self.n)

        def behind(self, d):
            return lax.rem(self.me + self.n - d, self.n)

        def spread(self, at):
            def go():
                for d in far_first(self.n):
                    rc(at(self.me), at(self.me), self.base + d, self.base + self.me, self.devof(self.ahead(d))).start()

            self.guarded(self.me, go)

            def drain():
                def fin():
                    for d in far_first(self.n):
                        rc(at(self.me), at(self.me), self.base + d, self.base + self.me, self.devof(self.ahead(d))).wait_send()

                self.guarded(self.me, fin)

            drains.append(drain)

        def gathered(self, at):
            for d in reversed(far_first(self.n)):
                q = self.behind(d)

                def fin(d=d, q=q):
                    rc(at(q), at(q), self.base + d, self.base + q, self.devof(q)).wait_recv()

                self.guarded(q, fin)

        def scatter(self, src, dst):
            def each(method):
                for d in far_first(self.n):
                    p = self.ahead(d)

                    def go(d=d, p=p):
                        getattr(rc(src(p), dst(self.me), self.base + d, self.base + self.me, self.devof(p)), method)()

                    self.guarded(p, go)

            each("start")
            drains.append(lambda: each("wait_send"))

        def scattered(self, dst):
            for d in reversed(far_first(self.n)):
                q = self.behind(d)
                rc(dst(q), dst(q), self.base + d, self.base + q, self.devof(q)).wait_recv()

    hload = [pltpu.make_async_copy(h_hbm.at[:, pl.ds(i * 2 * RB, 2 * RB)], hf.at[i], hsem.at[i]) for i in range(X)]
    for c in hload:
        c.start()

    barrier = pltpu.get_barrier_semaphore()

    def greet(to):
        pl.semaphore_signal(barrier, inc=1, device_id=to, device_id_type=MESH)

    for d in range(1, Z):
        greet(zdev(lax.rem(z + d, Z)))
    for d in range(1, Y):
        greet(ydev(lax.rem(y + d, Y)))
    for d in range(1, X):
        greet(xdev(lax.rem(x + d, X)))
    greet(partner)

    centre = (up[0] + lo[0]) * 0.5
    half_width = (up[0] - lo[0]) * 0.5
    inv_hw = 1.0 / half_width

    def prow(x_, c_, y_):
        return pall.at[pl.ds(pl.multiple_of(((x_ * 2 + c_) * Y + y_) * PR, 8), PR)]

    def pblk(x_, c_):
        return pall.at[pl.ds(pl.multiple_of((x_ * 2 + c_) * Y * PR, 8), Y * PR)]

    class Plane:
        def __init__(self, blk, piece, ya):
            self.xa = Axis(X, x, xdev, X)
            self.cbase = alloc(X)
            self.blk, self.piece, self.ya = blk, piece, ya

        def to_partner(self, q, method):
            getattr(rc(self.blk(q, core), self.blk(q, core), self.cbase + q, self.cbase + q, partner), method)()

        def forward(self, q):
            at, xa = self.piece(q), self.xa
            for d in far_first(X):
                rc(at, at, xa.base + d, xa.base + x, xdev(xa.ahead(d))).start()
            rc(at, at, self.cbase + x, self.cbase + x, partner).start()

        def collect(self):
            ya, xa = self.ya, self.xa
            ya.spread(self.piece)
            ya.guarded(y, lambda: self.forward(y))
            for d in reversed(far_first(Y)):
                q = ya.behind(d)

                def on(d=d, q=q):
                    rc(self.piece(q), self.piece(q), ya.base + d, ya.base + q, ydev(q)).wait_recv()
                    self.forward(q)

                ya.guarded(q, on)

            def drain():
                for d in far_first(X):
                    rc(self.blk(x, core), self.blk(x, core), xa.base + d, xa.base + x, xdev(xa.ahead(d))).wait_send()

            drains.append(drain)

        def relay(self):
            for d in reversed(far_first(X)):
                q = self.xa.behind(d)
                rc(self.blk(q, core), self.blk(q, core), self.xa.base + d, self.xa.base + q, xdev(q)).wait_recv()
                self.to_partner(q, "start")

            def drain():
                for q in range(X):
                    self.to_partner(q, "wait_send")

            drains.append(drain)

        def other_half(self, q):
            rc(self.blk(q, other), self.blk(q, other), self.cbase + q, self.cbase + q, partner).wait_recv()

    def split_h(i):
        hload[i].wait()
        diagonal = (y == z).astype(jnp.int32) * (x == i).astype(jnp.int32)
        off = core * RB - (1 - diagonal) * (8 * RB)

        hfi, hci = hf.at[i], hcat.at[i]

        @pl.loop(0, RB // 16)
        def _(t):
            row = pl.multiple_of(t * 16, 16)
            h = hfi[pl.ds(row, 16), :]
            ri = lax.broadcasted_iota(jnp.int32, h.shape, 0) + row
            ci = lax.broadcasted_iota(jnp.int32, h.shape, 1)
            h = jnp.where(ci - ri == off, h - centre, h)
            hi = h.astype(BF16)
            hci[pl.ds(row, 16), :] = hi
            hci[pl.ds(pl.multiple_of(row + RB, 16), 16), :] = (h - hi.astype(F32)).astype(BF16)

    prow(x, core, y)[...] = pk[...]
    for i in range(X // 2):
        split_h(i)
    pl.semaphore_wait(barrier, (Z - 1) + (Y - 1) + (X - 1) + 1)
    s0p = Plane(pblk, lambda q: prow(x, core, q), Axis(Y, y, ydev, Y))
    s0p.collect()
    for i in range(X // 2, X):
        split_h(i)
    s0p.relay()
    for q in range(X):
        s0p.other_half(q)

    @pl.loop(0, RB // 8)
    def _(t):
        for u in range(8):
            picked[pl.ds(t * 8 + u, 1), :] = pall[pl.ds(idx[t * 8 + u], 1), :]

    lane = lax.broadcasted_iota(jnp.int32, (RB, 128), 1)
    mine = jnp.where(lane // 8 == amod[...], picked[...], 0.0)
    fold = (lax.broadcasted_iota(jnp.int32, (8, 128), 1) % 8 == lax.broadcasted_iota(jnp.int32, (8, 128), 0)).astype(F32)
    z0[z] = nt(fold, mine)
    s1 = Axis(Z, z, zdev, Z)
    s1.spread(lambda q: z0.at[q])
    s1.gathered(lambda q: z0.at[q])
    for g in range(Z):
        xr0[pl.ds(g * W, W), :] = z0[g][:W, :]

    def cat(v):
        hi = v.astype(BF16).astype(F32)
        return jnp.concatenate([hi, v - hi], axis=0).astype(BF16)

    dxs = far_first(X)

    class Wide:
        def __init__(self, i):
            self.i = i
            self.cbase = alloc(X)
            self.xa = Axis(X, x, xdev, X)
            self.ya = Axis(Y, y, ydev, G)

        def pc(self, q, method):
            i = self.i
            getattr(rc(qb.at[i, q, other], cb.at[i, q], self.cbase + q, self.cbase + q, partner), method)()

        def multiply(self, v):
            i = self.i
            c2 = cat(v)
            lhs[:, :RB] = c2
            lhs[:, RB:] = c2

            @pl.loop(0, X)
            def _(k):
                q = lax.rem(x + pick(k, dxs + [0]), X)
                p = jnp.dot(lhs[...], hcat[q], preferred_element_type=F32)
                p = p[:K] + p[K:]
                qb[i, q, 0] = p[:, :RB].reshape(G, 8, RB)
                qb[i, q, 1] = p[:, RB:].reshape(G, 8, RB)
                self.pc(q, "start")

            drains.append(lambda: [self.pc(q, "wait_send") for q in range(X)])

        def pair(self, q):
            i = self.i
            rc(cb.at[i, q], cb.at[i, q], self.cbase + q, self.cbase + q, partner).wait_recv()
            return qb[i, q, core] + cb[i, q]

        def across(self):
            i, xa = self.i, self.xa

            def cp(d):
                q = xa.ahead(d)
                return rc(sb.at[i, q], xb.at[i, x], xa.base + d, xa.base + x, xdev(q))

            for d in dxs:
                q = xa.ahead(d)
                sb[i, q] = self.pair(q)
                cp(d).start()
            drains.append(lambda: [cp(d).wait_send() for d in dxs])

        def down(self):
            i = self.i
            total = self.pair(x)
            self.xa.scattered(lambda q: xb.at[i, q])
            for d in dxs:
                total = total + xb[i, self.xa.behind(d)]
            ysum[i] = total
            self.ya.scatter(lambda q: ysum.at[i, q], lambda q: yb.at[i, q])

        def chunk(self):
            i = self.i
            yb[i, y] = ysum[i, y]
            self.ya.scattered(lambda q: yb.at[i, q])
            total = yb[i, 0]
            for q in range(1, Y):
                total = total + yb[i, q]
            return total

    class Gather:
        def __init__(self, i):
            self.i = i
            self.ya = Axis(Y, y, ydev, G)
            self.plane = Plane(lambda q, c: XC.at[i, q, c], lambda q: XC.at[i, x, core, q], self.ya)

        def run(self):
            self.plane.collect()
            self.plane.relay()

    class Tall:
        def __init__(self, i):
            self.i = i
            self.rs = Axis(Z, z, zdev, G)
            self.ag = Axis(Z, z, zdev, G)

        def multiply(self, plane):
            i = self.i
            acc[...] = jnp.zeros_like(acc)

            @pl.loop(0, X)
            def _(k):
                q = lax.rem(x + pick(k, [0] + dxs[::-1]), X)
                plane.other_half(q)
                v = jnp.concatenate([XC[i, q, 0].reshape(K, RB), XC[i, q, 1].reshape(K, RB)], axis=1)
                acc[...] += lax.dot_general(cat(v), hcat[q], (((1,), (1,)), ((), ())), preferred_element_type=F32)

            a = acc[...]
            t = a[:K] + a[K:]
            t = t[:, :RB] + t[:, RB:]
            zsum[i] = t.reshape(G, 8, RB)
            self.rs.scatter(lambda q: zsum.at[i, q], lambda q: zb.at[i, q])

        def chunk(self):
            i = self.i
            zb[i, z] = zsum[i, z]
            self.rs.scattered(lambda q: zb.at[i, q])
            total = zb[i, 0]
            for q in range(1, Z):
                total = total + zb[i, q]
            return total

        def run(self):
            i = self.i
            self.ag.spread(lambda q: XR.at[i, q])
            self.ag.gathered(lambda q: XR.at[i, q])

    w0, w1, w2 = Wide(0), Wide(1), Wide(2)
    g0, g1 = Gather(0), Gather(1)
    t0, t1 = Tall(0), Tall(1)

    w0.multiply(xr0[...])
    w0.across()
    w0.down()

    @pl.when(y < G)
    def _():
        v = w0.chunk() * inv_hw
        f1[...] = v
        XC[0, x, core, y] = v

    g0.run()
    t0.multiply(g0.plane)

    @pl.when(z < G)
    def _():
        v = 2.0 * inv_hw * t0.chunk() - xr0[pl.ds(pl.multiple_of(z * 8, 8), 8), :]
        f2[...] = v
        XR[0, z] = v

    t0.run()
    w1.multiply(XR[0].reshape(K, RB))
    w1.across()
    w1.down()

    @pl.when(y < G)
    def _():
        XC[1, x, core, y] = 2.0 * inv_hw * w1.chunk() - f1[...]

    g1.run()
    t1.multiply(g1.plane)

    class Guard:
        def __init__(self, cond):
            self.cond = cond

        def __call__(self, fn):
            before = len(drains)
            pl.when(self.cond)(fn)
            late = drains[before:]
            del drains[before:]

            def drain():
                def fin():
                    for f in late:
                        f()

                pl.when(self.cond)(fin)

            drains.append(drain)

    gown, pown = Guard(z < G), Guard(y < G)
    tya, tza = Axis(Y, y, ydev, Y), Axis(Z, z, zdev, G)

    @gown
    def _():
        v = 2.0 * inv_hw * t1.chunk() - f2[...]
        XR[1, z] = v
        yt[y] = v

    t1.ag.spread(lambda q: XR.at[1, q])
    gown(lambda: tya.spread(lambda q: yt.at[q]))
    t1.ag.gathered(lambda q: XR.at[1, q])

    w2.multiply(XR[1].reshape(K, RB))

    gay, gax, gaz = Axis(Y, y, ydev, Y), Axis(X, x, xdev, X), Axis(Z, z, zdev, G)
    paz, pax, pay = Axis(Z, z, zdev, Z), Axis(X, x, xdev, X), Axis(Y, y, ydev, G)
    gcb, pcb = alloc(1), alloc(1)

    def widen(v):
        return jnp.concatenate([v, jnp.zeros((8, 128 - K), F32)], axis=1)

    def total_of(ref, n):
        t = ref[0]
        for q in range(1, n):
            t = t + ref[q]
        return t

    def swap_cores(ref, base):
        cp = lambda: rc(ref.at[core], ref.at[core], base, base, partner)
        cp().start()
        drains.append(lambda: cp().wait_send())

    def swapped(ref, base):
        rc(ref.at[other], ref.at[other], base, base, partner).wait_recv()

    @gown
    def _():
        gy[y] = widen(nt(XR[1, z], XR[1].reshape(K, RB)))
        gay.spread(lambda q: gy.at[q])

    w2.across()

    def turn(d):
        p = tza.ahead(d)
        return rc(yt.at[p], XT.at[z], tza.base + d, tza.base + z, zdev(p))

    @gown
    def _():
        tya.gathered(lambda q: yt.at[q])
        for d in far_first(Z):
            turn(d).start()
        drains.append(lambda: [turn(d).wait_send() for d in far_first(Z)])
        XT[z] = yt[z]
        gay.gathered(lambda q: gy.at[q])
        gx[x] = total_of(gy, Y)
        gax.spread(lambda q: gx.at[q])

    w2.down()

    @gown
    def _():
        gax.gathered(lambda q: gx.at[q])
        gc[core] = total_of(gx, X)
        swap_cores(gc, gcb)

    @gown
    def _():
        swapped(gc, gcb)
        gz[z] = gc[0] + gc[1]

    gaz.spread(lambda q: gz.at[q])
    tza.gathered(lambda q: XT.at[q])

    @pown
    def _():
        pz[z] = widen(nt(w2.chunk(), XT[...].reshape(K, RB)))
        paz.spread(lambda q: pz.at[q])

    gaz.gathered(lambda q: gz.at[q])
    gram = gz[...].reshape(K, 128)[:, :K] * (1.0 / N)

    eye = (lax.broadcasted_iota(jnp.int32, (K, K), 0) == lax.broadcasted_iota(jnp.int32, (K, K), 1)).astype(F32)
    work = jnp.concatenate([gram, eye], axis=1)
    rows = lax.broadcasted_iota(jnp.int32, (K, 1), 0)
    scale = jnp.zeros((K, 1), F32)

    def eliminate(first, last, work, scale):
        for j in range(first, last):
            prow_ = work[j : j + 1, :]
            piv = work[j : j + 1, j : j + 1]
            col = work[:, j : j + 1]
            m = jnp.where(rows > j, col / piv, 0.0)
            scale = jnp.where(rows == j, piv, scale)
            work = work - m * prow_
        return work, scale

    work, scale = eliminate(0, K // 2, work, scale)

    @pown
    def _():
        paz.gathered(lambda q: pz.at[q])
        px[x] = total_of(pz, Z)
        pax.spread(lambda q: px.at[q])

    work, scale = eliminate(K // 2, 5 * K // 8, work, scale)

    @pown
    def _():
        pax.gathered(lambda q: px.at[q])
        pc[core] = total_of(px, X)
        swap_cores(pc, pcb)

    work, scale = eliminate(5 * K // 8, 3 * K // 4, work, scale)

    @pown
    def _():
        swapped(pc, pcb)
        py[y] = pc[0] + pc[1]

    pay.spread(lambda q: py.at[q])
    work, scale = eliminate(3 * K // 4, K, work, scale)
    inverse = work[:, K:] * lax.rsqrt(scale)
    inv_ref[...] = inverse
    own = inv_ref[pl.ds(z * W, W), :]
    basis_ref[...] = jnp.dot(own, XR[1].reshape(K, RB), precision=HIGHEST, preferred_element_type=F32)

    pay.gathered(lambda q: py.at[q])
    proj = py[...].reshape(K, 128)[:, :K] * (1.0 / N)
    proj = proj + centre * gram
    ritz_ref[...] = nt(nt(inverse, proj), inverse)

    for f in drains:
        f()


def body(hamiltonian, previous, correlation_map, lower_cut, upper_bound):
    Z = lax.axis_size("col")
    R = lax.axis_size("row")
    Y = Z
    X = R // (2 * Y)
    RB, W = previous.shape
    K = W * Z
    G = K // 8
    N = RB * R
    PR = RB // 16
    pk = jnp.pad(previous, ((0, 0), (0, 8 - W))).reshape(PR, 128)
    src = correlation_map // RB
    off = correlation_map % RB
    slot = (src % (2 * X)) * Y + src // (2 * X)
    idx = slot * PR + off // 16
    amod = (off % 16)[:, None]
    V, S = pltpu.VMEM, pltpu.SMEM
    blk = (G, 8, RB)
    scratch = [
        V((X, RB, 2 * RB), F32),
        V((X, 2 * RB, 2 * RB), BF16),
        V((R * PR, 128), F32),
        V((RB, 128), F32),
        V((Z, 8, RB), F32),
        V((K, RB), F32),
        V((2 * K, 2 * RB), BF16),
        V((2 * K, 2 * RB), F32),
        V((3, X, 2) + blk, F32),
        V((3, X) + blk, F32),
        V((3, X) + blk, F32),
        V((3, X) + blk, F32),
        V((3,) + blk, F32),
        V((3, Y, 8, RB), F32),
        V((2, X, 2) + blk, F32),
        V((8, RB), F32),
        V((2,) + blk, F32),
        V((2, Z, 8, RB), F32),
        V((2,) + blk, F32),
        V((8, RB), F32),
        V(blk, F32),
        V((Y, 8, RB), F32),
        V((Y, 8, 128), F32),
        V((X, 8, 128), F32),
        V((2, 8, 128), F32),
        V((G, 8, 128), F32),
        V((Z, 8, 128), F32),
        V((X, 8, 128), F32),
        V((2, 8, 128), F32),
        V((G, 8, 128), F32),
        V((K, K), F32),
        pltpu.SemaphoreType.DMA((X,)),
        pltpu.SemaphoreType.DMA((NSEM,)),
        pltpu.SemaphoreType.DMA((NSEM,)),
    ]
    vm = pl.BlockSpec(memory_space=V)
    sm = pl.BlockSpec(memory_space=S)
    basis_t, ritz = pl.pallas_call(
        lambda *refs: kernel(X, Y, Z, RB, K, N, *refs),
        out_shape=(jax.ShapeDtypeStruct((W, RB), F32), jax.ShapeDtypeStruct((K, K), F32)),
        in_specs=[pl.BlockSpec(memory_space=pl.ANY), vm, sm, vm, sm, sm],
        out_specs=(vm, vm),
        scratch_shapes=scratch,
        compiler_params=pltpu.CompilerParams(collective_id=0, has_side_effects=True, vmem_limit_bytes=60 * 1024 * 1024),
        name="subspace",
    )(hamiltonian, pk, idx, amod, lower_cut, upper_bound)
    return basis_t.T, ritz


def solution(mesh):
    return jax.shard_map(
        body,
        mesh=mesh,
        in_specs=(P("row", "col"), P("row", "col"), P("row"), P(), P()),
        out_specs=(P("row", "col"), P()),
        check_vma=False,
    )
```

```python
import jax
import jax.numpy as jnp
from jax import lax
from jax.experimental import pallas as pl
from jax.experimental.pallas import tpu as pltpu
from jax.sharding import PartitionSpec as P

MESH = pl.DeviceIdType.MESH
F32 = jnp.float32
BF16 = jnp.bfloat16
HIGHEST = lax.Precision.HIGHEST
NSEM = 224


def far_first(n):
    return sorted(range(1, n), key=lambda d: -min(d, n - d))


def pick(k, table):
    return sum((k == i).astype(jnp.int32) * t for i, t in enumerate(table) if t)


def nt(a, b):
    return lax.dot_general(a, b, (((1,), (1,)), ((), ())), precision=HIGHEST, preferred_element_type=F32)


def kernel(
    X, Y, Z, RB, K, N,
    h_hbm, pk, cmap, lo, up,
    basis_ref, ritz_ref,
    hf, hcat, pall, picked, z0, xr0, lhs, acc, qb, cb, sb, xb, ysum, yb, XC, f1,
    zsum, zb, XR, f2, XT, yt, gy, gx, gz, pz, px, py, inv_ref, pos,
    hsem, ssem, rsem,
):
    G = K // 8
    W = K // Z
    PR = RB // 16
    r = lax.axis_index("row")
    z = lax.axis_index("col")
    core = lax.rem(r, 2)
    x = lax.rem(r // 2, X)
    y = r // (2 * X)
    other = 1 - core

    def dev(x_, y_, c_, z_):
        return ((y_ * X + x_) * 2 + c_, z_)

    zdev = lambda q: dev(x, y, core, q)
    ydev = lambda q: dev(x, q, core, z)
    xdev = lambda q: dev(q, y, core, z)
    partner = dev(x, y, other, z)
    spot = x * 2 + core
    mdev = lambda m: dev(m // 2, y, lax.rem(m, 2), z)

    used = [0]
    drains = []

    def alloc(n):
        base = used[0]
        used[0] += n
        assert used[0] <= NSEM
        return base

    def rc(src, dst, si, ri, to):
        return pltpu.make_async_remote_copy(
            src_ref=src, dst_ref=dst, send_sem=ssem.at[si], recv_sem=rsem.at[ri], device_id=to, device_id_type=MESH
        )

    class Axis:
        def __init__(self, n, me, devof, owners):
            self.n, self.me, self.devof, self.owners = n, me, devof, owners
            self.base = alloc(n)

        def guarded(self, who, fn):
            if self.owners >= self.n:
                fn()
            else:
                pl.when(who < self.owners)(fn)

        def ahead(self, d):
            return lax.rem(self.me + d, self.n)

        def behind(self, d):
            return lax.rem(self.me + self.n - d, self.n)

        def spread(self, at):
            def go():
                for d in far_first(self.n):
                    rc(at(self.me), at(self.me), self.base + d, self.base + self.me, self.devof(self.ahead(d))).start()

            self.guarded(self.me, go)

            def drain():
                def fin():
                    for d in far_first(self.n):
                        rc(at(self.me), at(self.me), self.base + d, self.base + self.me, self.devof(self.ahead(d))).wait_send()

                self.guarded(self.me, fin)

            drains.append(drain)

        def gathered(self, at):
            for d in reversed(far_first(self.n)):
                q = self.behind(d)

                def fin(d=d, q=q):
                    rc(at(q), at(q), self.base + d, self.base + q, self.devof(q)).wait_recv()

                self.guarded(q, fin)

        def scatter(self, src, dst):
            def each(method):
                for d in far_first(self.n):
                    p = self.ahead(d)

                    def go(d=d, p=p):
                        getattr(rc(src(p), dst(self.me), self.base + d, self.base + self.me, self.devof(p)), method)()

                    self.guarded(p, go)

            each("start")
            drains.append(lambda: each("wait_send"))

        def scattered(self, dst):
            for d in reversed(far_first(self.n)):
                q = self.behind(d)
                rc(dst(q), dst(q), self.base + d, self.base + q, self.devof(q)).wait_recv()

    hload = [pltpu.make_async_copy(h_hbm.at[:, pl.ds(i * 2 * RB, 2 * RB)], hf.at[i], hsem.at[i]) for i in range(X)]
    for c in hload:
        c.start()

    barrier = pltpu.get_barrier_semaphore()

    def greet(to):
        pl.semaphore_signal(barrier, inc=1, device_id=to, device_id_type=MESH)

    for d in range(1, Z):
        greet(zdev(lax.rem(z + d, Z)))
    for d in range(1, Y):
        greet(ydev(lax.rem(y + d, Y)))
    for d in range(1, X):
        greet(xdev(lax.rem(x + d, X)))
        greet(dev(lax.rem(x + d, X), y, other, z))
    greet(partner)

    centre = (up[0] + lo[0]) * 0.5
    half_width = (up[0] - lo[0]) * 0.5
    inv_hw = 1.0 / half_width

    def prow(x_, c_, y_):
        return pall.at[pl.ds(pl.multiple_of(((x_ * 2 + c_) * Y + y_) * PR, 8), PR)]

    def pblk(x_, c_):
        return pall.at[pl.ds(pl.multiple_of((x_ * 2 + c_) * Y * PR, 8), Y * PR)]

    class Plane:
        def __init__(self, blk, piece, ya):
            self.xa = Axis(X, x, xdev, X)
            self.cbase = alloc(X)
            self.blk, self.piece, self.ya = blk, piece, ya

        def to_partner(self, q, method):
            getattr(rc(self.blk(q, core), self.blk(q, core), self.cbase + q, self.cbase + q, partner), method)()

        def forward(self, q):
            at, xa = self.piece(q), self.xa
            for d in far_first(X):
                rc(at, at, xa.base + d, xa.base + x, xdev(xa.ahead(d))).start()
            rc(at, at, self.cbase + x, self.cbase + x, partner).start()

        def collect(self):
            ya, xa = self.ya, self.xa
            ya.spread(self.piece)
            ya.guarded(y, lambda: self.forward(y))
            for d in reversed(far_first(Y)):
                q = ya.behind(d)

                def on(d=d, q=q):
                    rc(self.piece(q), self.piece(q), ya.base + d, ya.base + q, ydev(q)).wait_recv()
                    self.forward(q)

                ya.guarded(q, on)

            def drain():
                for d in far_first(X):
                    rc(self.blk(x, core), self.blk(x, core), xa.base + d, xa.base + x, xdev(xa.ahead(d))).wait_send()

            drains.append(drain)

        def relay(self):
            for d in reversed(far_first(X)):
                q = self.xa.behind(d)
                rc(self.blk(q, core), self.blk(q, core), self.xa.base + d, self.xa.base + q, xdev(q)).wait_recv()
                self.to_partner(q, "start")

            def drain():
                for q in range(X):
                    self.to_partner(q, "wait_send")

            drains.append(drain)

        def other_half(self, q):
            rc(self.blk(q, other), self.blk(q, other), self.cbase + q, self.cbase + q, partner).wait_recv()

    def split_h(i):
        hload[i].wait()
        diagonal = (y == z).astype(jnp.int32) * (x == i).astype(jnp.int32)
        off = core * RB - (1 - diagonal) * (8 * RB)

        hfi, hci = hf.at[i], hcat.at[i]

        @pl.loop(0, RB // 16)
        def _(t):
            row = pl.multiple_of(t * 16, 16)
            h = hfi[pl.ds(row, 16), :]
            ri = lax.broadcasted_iota(jnp.int32, h.shape, 0) + row
            ci = lax.broadcasted_iota(jnp.int32, h.shape, 1)
            h = jnp.where(ci - ri == off, h - centre, h)
            hi = h.astype(BF16)
            hci[pl.ds(row, 16), :] = hi
            hci[pl.ds(pl.multiple_of(row + RB, 16), 16), :] = (h - hi.astype(F32)).astype(BF16)

    prow(x, core, y)[...] = pk[...]
    for i in range(X // 2):
        split_h(i)
    pl.semaphore_wait(barrier, (Z - 1) + (Y - 1) + 2 * (X - 1) + 1)
    s0p = Plane(pblk, lambda q: prow(x, core, q), Axis(Y, y, ydev, Y))
    s0p.collect()
    for i in range(X // 2, X):
        split_h(i)

    recip = -(-65536 // PR)

    @pl.loop(0, RB // 8)
    def _(t):
        for u in range(8):
            row = lax.shift_right_logical(cmap[t * 8 + u], 4)
            src = lax.shift_right_logical(row * recip, 16)
            slot = (src & (2 * X - 1)) * Y + lax.shift_right_logical(src, (2 * X).bit_length() - 1)
            pos[t * 8 + u] = slot * PR + row - src * PR

    s0p.relay()
    for q in range(X):
        s0p.other_half(q)
    group = lax.broadcasted_iota(jnp.int32, (1, 128), 1) // 8

    @pl.loop(0, RB // 8)
    def _(t):
        for u in range(8):
            i = t * 8 + u
            picked[pl.ds(i, 1), :] = jnp.where(group == (cmap[i] & 15), pall[pl.ds(pos[i], 1), :], 0.0)

    fold = (lax.broadcasted_iota(jnp.int32, (8, 128), 1) % 8 == lax.broadcasted_iota(jnp.int32, (8, 128), 0)).astype(F32)
    z0[z] = nt(fold, picked[...])
    s1 = Axis(Z, z, zdev, Z)
    s1.spread(lambda q: z0.at[q])
    s1.gathered(lambda q: z0.at[q])
    for g in range(Z):
        xr0[pl.ds(g * W, W), :] = z0[g][:W, :]

    def cat(v):
        hi = v.astype(BF16).astype(F32)
        return jnp.concatenate([hi, v - hi], axis=0).astype(BF16)

    dxs = far_first(X)

    class Wide:
        def __init__(self, i):
            self.i = i
            self.cbase = alloc(X)
            self.xa = Axis(X, x, xdev, X)
            self.ya = Axis(Y, y, ydev, G)

        def pc(self, q, method):
            i = self.i
            getattr(rc(qb.at[i, q, other], cb.at[i, q], self.cbase + q, self.cbase + q, partner), method)()

        def multiply(self, v):
            i = self.i
            c2 = cat(v)
            lhs[:, :RB] = c2
            lhs[:, RB:] = c2

            @pl.loop(0, X)
            def _(k):
                q = lax.rem(x + pick(k, dxs + [0]), X)
                p = jnp.dot(lhs[...], hcat[q], preferred_element_type=F32)
                p = p[:K] + p[K:]
                qb[i, q, 0] = p[:, :RB].reshape(G, 8, RB)
                qb[i, q, 1] = p[:, RB:].reshape(G, 8, RB)
                self.pc(q, "start")

            drains.append(lambda: [self.pc(q, "wait_send") for q in range(X)])

        def pair(self, q):
            i = self.i
            rc(cb.at[i, q], cb.at[i, q], self.cbase + q, self.cbase + q, partner).wait_recv()
            return qb[i, q, core] + cb[i, q]

        def across(self):
            i, xa = self.i, self.xa

            def cp(d):
                q = xa.ahead(d)
                return rc(sb.at[i, q], xb.at[i, x], xa.base + d, xa.base + x, xdev(q))

            for d in dxs:
                q = xa.ahead(d)
                sb[i, q] = self.pair(q)
                cp(d).start()
            drains.append(lambda: [cp(d).wait_send() for d in dxs])

        def down(self):
            i = self.i
            total = self.pair(x)
            self.xa.scattered(lambda q: xb.at[i, q])
            for d in dxs:
                total = total + xb[i, self.xa.behind(d)]
            ysum[i] = total
            self.ya.scatter(lambda q: ysum.at[i, q], lambda q: yb.at[i, q])

        def chunk(self):
            i = self.i
            yb[i, y] = ysum[i, y]
            self.ya.scattered(lambda q: yb.at[i, q])
            total = yb[i, 0]
            for q in range(1, Y):
                total = total + yb[i, q]
            return total

    class Gather:
        def __init__(self, i):
            self.i = i
            self.ya = Axis(Y, y, ydev, G)
            self.plane = Plane(lambda q, c: XC.at[i, q, c], lambda q: XC.at[i, x, core, q], self.ya)

        def run(self):
            self.plane.collect()
            self.plane.relay()

    class Tall:
        def __init__(self, i):
            self.i = i
            self.rs = Axis(Z, z, zdev, G)
            self.ag = Axis(Z, z, zdev, G)

        def multiply(self, plane):
            i = self.i
            acc[...] = jnp.zeros_like(acc)

            @pl.loop(0, X)
            def _(k):
                q = lax.rem(x + pick(k, [0] + dxs[::-1]), X)
                plane.other_half(q)
                v = jnp.concatenate([XC[i, q, 0].reshape(K, RB), XC[i, q, 1].reshape(K, RB)], axis=1)
                acc[...] += lax.dot_general(cat(v), hcat[q], (((1,), (1,)), ((), ())), preferred_element_type=F32)

            a = acc[...]
            t = a[:K] + a[K:]
            t = t[:, :RB] + t[:, RB:]
            zsum[i] = t.reshape(G, 8, RB)
            self.rs.scatter(lambda q: zsum.at[i, q], lambda q: zb.at[i, q])

        def chunk(self):
            i = self.i
            zb[i, z] = zsum[i, z]
            self.rs.scattered(lambda q: zb.at[i, q])
            total = zb[i, 0]
            for q in range(1, Z):
                total = total + zb[i, q]
            return total

        def run(self):
            i = self.i
            self.ag.spread(lambda q: XR.at[i, q])
            self.ag.gathered(lambda q: XR.at[i, q])

    w0, w1, w2 = Wide(0), Wide(1), Wide(2)
    g0, g1 = Gather(0), Gather(1)
    t0, t1 = Tall(0), Tall(1)

    w0.multiply(xr0[...])
    w0.across()
    w0.down()

    @pl.when(y < G)
    def _():
        v = w0.chunk() * inv_hw
        f1[...] = v
        XC[0, x, core, y] = v

    g0.run()
    t0.multiply(g0.plane)

    @pl.when(z < G)
    def _():
        v = 2.0 * inv_hw * t0.chunk() - xr0[pl.ds(pl.multiple_of(z * 8, 8), 8), :]
        f2[...] = v
        XR[0, z] = v

    t0.run()
    w1.multiply(XR[0].reshape(K, RB))
    w1.across()
    w1.down()

    @pl.when(y < G)
    def _():
        XC[1, x, core, y] = 2.0 * inv_hw * w1.chunk() - f1[...]

    g1.run()
    t1.multiply(g1.plane)

    class Guard:
        def __init__(self, cond):
            self.cond = cond

        def __call__(self, fn):
            before = len(drains)
            pl.when(self.cond)(fn)
            late = drains[before:]
            del drains[before:]

            def drain():
                def fin():
                    for f in late:
                        f()

                pl.when(self.cond)(fin)

            drains.append(drain)

    gown, pown = Guard(z < G), Guard(y < G)
    tya, tza = Axis(Y, y, ydev, Y), Axis(Z, z, zdev, G)

    @gown
    def _():
        v = 2.0 * inv_hw * t1.chunk() - f2[...]
        XR[1, z] = v
        yt[y] = v

    t1.ag.spread(lambda q: XR.at[1, q])
    gown(lambda: tya.spread(lambda q: yt.at[q]))
    t1.ag.gathered(lambda q: XR.at[1, q])

    w2.multiply(XR[1].reshape(K, RB))

    gay, gax, gaz = Axis(Y, y, ydev, Y), Axis(2 * X, spot, mdev, 2 * X), Axis(Z, z, zdev, G)
    paz, pax, pay = Axis(Z, z, zdev, Z), Axis(2 * X, spot, mdev, 2 * X), Axis(Y, y, ydev, G)

    def widen(v):
        return jnp.concatenate([v, jnp.zeros((8, 128 - K), F32)], axis=1)

    def total_of(ref, n):
        t = ref[0]
        for q in range(1, n):
            t = t + ref[q]
        return t

    @gown
    def _():
        gy[y] = widen(nt(XR[1, z], XR[1].reshape(K, RB)))
        gay.spread(lambda q: gy.at[q])

    w2.across()

    def turn(d):
        p = tza.ahead(d)
        return rc(yt.at[p], XT.at[z], tza.base + d, tza.base + z, zdev(p))

    @gown
    def _():
        tya.gathered(lambda q: yt.at[q])
        for d in far_first(Z):
            turn(d).start()
        drains.append(lambda: [turn(d).wait_send() for d in far_first(Z)])
        XT[z] = yt[z]
        gay.gathered(lambda q: gy.at[q])
        gx[spot] = total_of(gy, Y)
        gax.spread(lambda q: gx.at[q])

    w2.down()

    @gown
    def _():
        gax.gathered(lambda q: gx.at[q])
        gz[z] = total_of(gx, 2 * X)

    gaz.spread(lambda q: gz.at[q])
    tza.gathered(lambda q: XT.at[q])

    @pown
    def _():
        pz[z] = widen(nt(w2.chunk(), XT[...].reshape(K, RB)))
        paz.spread(lambda q: pz.at[q])

    gaz.gathered(lambda q: gz.at[q])
    gram = gz[...].reshape(K, 128)[:, :K] * (1.0 / N)

    eye = (lax.broadcasted_iota(jnp.int32, (K, K), 0) == lax.broadcasted_iota(jnp.int32, (K, K), 1)).astype(F32)
    work = jnp.concatenate([gram, eye], axis=1)
    rows = lax.broadcasted_iota(jnp.int32, (K, 1), 0)
    scale = jnp.zeros((K, 1), F32)

    def eliminate(first, last, work, scale):
        for j in range(first, last):
            prow_ = work[j : j + 1, :]
            piv = work[j : j + 1, j : j + 1]
            col = work[:, j : j + 1]
            m = jnp.where(rows > j, col / piv, 0.0)
            scale = jnp.where(rows == j, piv, scale)
            work = work - m * prow_
        return work, scale

    work, scale = eliminate(0, K // 2, work, scale)

    @pown
    def _():
        paz.gathered(lambda q: pz.at[q])
        px[spot] = total_of(pz, Z)
        pax.spread(lambda q: px.at[q])

    work, scale = eliminate(K // 2, 5 * K // 8, work, scale)

    @pown
    def _():
        pax.gathered(lambda q: px.at[q])
        py[y] = total_of(px, 2 * X)

    pay.spread(lambda q: py.at[q])
    work, scale = eliminate(5 * K // 8, K, work, scale)
    inverse = work[:, K:] * lax.rsqrt(scale)
    inv_ref[...] = inverse
    own = inv_ref[pl.ds(z * W, W), :]
    basis_ref[...] = jnp.dot(own, XR[1].reshape(K, RB), precision=HIGHEST, preferred_element_type=F32)

    pay.gathered(lambda q: py.at[q])
    proj = py[...].reshape(K, 128)[:, :K] * (1.0 / N)
    proj = proj + centre * gram
    ritz_ref[...] = nt(nt(inverse, proj), inverse)

    for f in drains:
        f()


def body(hamiltonian, previous, correlation_map, lower_cut, upper_bound):
    Z = lax.axis_size("col")
    R = lax.axis_size("row")
    Y = Z
    X = R // (2 * Y)
    RB, W = previous.shape
    K = W * Z
    G = K // 8
    N = RB * R
    PR = RB // 16
    pk = jnp.pad(previous, ((0, 0), (0, 8 - W))).reshape(PR, 128)
    V, S = pltpu.VMEM, pltpu.SMEM
    blk = (G, 8, RB)
    scratch = [
        V((X, RB, 2 * RB), F32),
        V((X, 2 * RB, 2 * RB), BF16),
        V((R * PR, 128), F32),
        V((RB, 128), F32),
        V((Z, 8, RB), F32),
        V((K, RB), F32),
        V((2 * K, 2 * RB), BF16),
        V((2 * K, 2 * RB), F32),
        V((3, X, 2) + blk, F32),
        V((3, X) + blk, F32),
        V((3, X) + blk, F32),
        V((3, X) + blk, F32),
        V((3,) + blk, F32),
        V((3, Y, 8, RB), F32),
        V((2, X, 2) + blk, F32),
        V((8, RB), F32),
        V((2,) + blk, F32),
        V((2, Z, 8, RB), F32),
        V((2,) + blk, F32),
        V((8, RB), F32),
        V(blk, F32),
        V((Y, 8, RB), F32),
        V((Y, 8, 128), F32),
        V((2 * X, 8, 128), F32),
        V((G, 8, 128), F32),
        V((Z, 8, 128), F32),
        V((2 * X, 8, 128), F32),
        V((G, 8, 128), F32),
        V((K, K), F32),
        S((RB,), jnp.int32),
        pltpu.SemaphoreType.DMA((X,)),
        pltpu.SemaphoreType.DMA((NSEM,)),
        pltpu.SemaphoreType.DMA((NSEM,)),
    ]
    vm = pl.BlockSpec(memory_space=V)
    sm = pl.BlockSpec(memory_space=S)
    basis_t, ritz = pl.pallas_call(
        lambda *refs: kernel(X, Y, Z, RB, K, N, *refs),
        out_shape=(jax.ShapeDtypeStruct((W, RB), F32), jax.ShapeDtypeStruct((K, K), F32)),
        in_specs=[pl.BlockSpec(memory_space=pl.ANY), vm, sm, sm, sm],
        out_specs=(vm, vm),
        scratch_shapes=scratch,
        compiler_params=pltpu.CompilerParams(collective_id=0, has_side_effects=True, vmem_limit_bytes=60 * 1024 * 1024),
        name="subspace",
    )(hamiltonian, pk, correlation_map, lower_cut, upper_bound)
    return basis_t.T, ritz


def solution(mesh):
    return jax.shard_map(
        body,
        mesh=mesh,
        in_specs=(P("row", "col"), P("row", "col"), P("row"), P(), P()),
        out_specs=(P("row", "col"), P()),
        check_vma=False,
    )
```
